32 devices in a mesh: fsdp: 32 (over z, y, x, core).
Axes of the slice: x: 2, y: 2, z: 4, core: 2. Of those that a mesh axis runs over, the one named last changes fastest.
Arguments:
- inputs: bfloat16 [32, 128, 768], P('fsdp'), may hold values from -6 to 6
- encoded: bfloat16 [32, 64, 768], P('fsdp')
- lengths: int32 [32], P('fsdp'), may hold values from 32 to 128, as said below
- bucket_ids: int32 [128], replicated, may hold values from 0 to 31, as said below
- qkv_weights: bfloat16 [768, 6, 768], P('fsdp')
- out_weights: bfloat16 [768, 2, 768], P('fsdp'), may hold values from -1.75 to 1.75
- ff_in: bfloat16 [768, 2, 2048], P('fsdp'), may hold values from -0.21875 to 0.21875
- ff_out: bfloat16 [2048, 768], P('fsdp'), may hold values from -0.125 to 0.125
- gains: bfloat16 [3, 768], P(None, 'fsdp'), may hold values from 0.5 to 1.5
- bias_table: float32 [32, 12], replicated
- cotangent: bfloat16 [32, 128, 768], P('fsdp'), may hold values from -6 to 6
Outputs:
- outputs: bfloat16 [32, 128, 768], P('fsdp')
- input_grad: bfloat16 [32, 128, 768], P('fsdp')
- encoded_grad: bfloat16 [32, 64, 768], P('fsdp')
- qkv_grad: float32 [768, 6, 768], P('fsdp')
- out_grad: float32 [768, 2, 768], P('fsdp')
- ffin_grad: float32 [768, 2, 2048], P('fsdp')
- ffout_grad: float32 [2048, 768], P('fsdp')
- gain_grad: float32 [3, 768], P(None, 'fsdp')
- table_grad: float32 [32, 12], replicated
The draws below stay inside these ranges and needn't reach their ends.
Inputs may be any that keep to these rules, and one draw needn't show every extreme that they name: `lengths`: some sequence uses all 128 slots. `bucket_ids`: non-decreasing in the distance; distance 0 has bucket 0 and distance 128 - 1 bucket 32 - 1.
All inputs are finite; a program needn't handle non-finite values.
Results may differ from the reference program's by a relative error of at most 0.02.
Values may be sent and summed in bfloat16 or wider, within the bound.
A program may use at most 192 MiB of HBM per device.

```python
import jax
import jax.numpy as jnp
from jax import lax

D = 768
HEADS = 12
HEAD = 64
FF = 2048
NB = 32
L = 128
E = 64
SEQS = 32


def draw_lengths(key, part):
    values = jax.random.randint(key, (SEQS,), L // 4, L + 1).astype(jnp.int32)
    return values.at[0].set(L)


def draw_bucket_ids(key, part):
    steps = jax.random.randint(key, (L,), 0, 2).astype(jnp.int32)
    steps = steps.at[0].set(0)
    buckets = jnp.minimum(jnp.cumsum(steps), NB - 1).astype(jnp.int32)
    return buckets.at[L - 1].set(NB - 1)


def draw_qkv_weights(key, part):
    values = jnp.clip(jax.random.normal(key, (D, 6, D), jnp.float32), -6.0, 6.0)
    which = jnp.arange(6, dtype=jnp.int32)
    query_like = (which == 0) | (which == 3)
    factor = jnp.where(query_like, (D * HEAD) ** (-0.5), D ** (-0.5)).astype(jnp.float32)
    return (values * factor[None, :, None]).astype(jnp.bfloat16)


def draw_encoded(key, part):
    values = jnp.clip(jax.random.normal(key, (SEQS, E, D), jnp.float32), -6.0, 6.0)
    return values.astype(jnp.bfloat16)


def draw_bias_table(key, part):
    values = jnp.clip(jax.random.normal(key, (NB, HEADS), jnp.float32), -4.0, 4.0)
    return values.astype(jnp.float32)


def block_scale(rng, dims, pieces, low, top_value):
    level = 1.0
    for position, parts in pieces:
        steps = jax.random.uniform(jax.random.fold_in(jax.random.fold_in(rng, 6), position), (parts,), jnp.float32, low / len(pieces), top_value / len(pieces))
        level = level * jnp.repeat(jnp.exp(steps), dims[position] // parts).reshape((-1,) + (1,) * (len(dims) - 1 - position))
    return level


def bell_draw(key, dims, width, most, shards=(), kind=jnp.bfloat16):
    values = width * jax.random.normal(key, dims, jnp.float32)
    if shards:
        values = values * block_scale(key, dims, shards, -0.22, 0.18)
    return jnp.clip(values, -most, most).astype(kind)


def setup_inputs(seed: int = 0) -> dict:
    streams_of = jax.random.split(jax.random.key(seed), 12)
    inputs = bell_draw(streams_of[0], (SEQS, L, D), 1.0, 6.0, ((0, 32),))
    encoded = draw_encoded(jax.random.fold_in(streams_of[11], 71), 0)
    lengths = draw_lengths(jax.random.fold_in(streams_of[11], 71), 0)
    bucket_ids = draw_bucket_ids(jax.random.fold_in(streams_of[11], 71), 0)
    qkv_weights = draw_qkv_weights(jax.random.fold_in(streams_of[11], 71), 0)
    out_weights = bell_draw(streams_of[5], (D, 2, D), (D // 64) ** -0.5, 1.75, ((0, 32),))
    ff_in = bell_draw(streams_of[6], (D, 2, FF), D ** -0.5, 0.21875, ((0, 32),))
    ff_out = bell_draw(streams_of[7], (FF, D), FF ** -0.5, 0.125, ((0, 32),))
    gains = jnp.clip(1.0 + 0.1 * jax.random.normal(streams_of[8], (3, D), jnp.float32), 0.5, 1.5).astype(jnp.bfloat16)
    bias_table = draw_bias_table(jax.random.fold_in(streams_of[11], 71), 0)
    cotangent = bell_draw(streams_of[10], (SEQS, L, D), 1.0, 6.0, ((0, 32),))
    return {"inputs": inputs, "encoded": encoded, "lengths": lengths, "bucket_ids": bucket_ids, "qkv_weights": qkv_weights, "out_weights": out_weights, "ff_in": ff_in, "ff_out": ff_out, "gains": gains, "bias_table": bias_table, "cotangent": cotangent}


EPS = 1e-06

def prod(form, left, right):
    return jnp.einsum(form, left.astype(jnp.float32), right.astype(jnp.float32))

def gelu_tanh(value):
    return 0.5 * value * (1.0 + jnp.tanh(0.7978845608028654 * (value + 0.044715 * value * value * value)))

def rms_fwd(value, gain):
    recip = lax.rsqrt(lax.optimization_barrier(jnp.mean(value * value, axis=-1, keepdims=True)) + EPS)
    normed = value * recip
    return ((normed * gain).astype(jnp.bfloat16), normed, recip)

def rms_bwd(grad, normed, recip, gain):
    scaled = grad * gain
    gain_grad = lax.optimization_barrier(jnp.sum(grad * normed, axis=0))
    back = recip * (scaled - normed * lax.optimization_barrier(jnp.mean(scaled * normed, axis=-1, keepdims=True)))
    return (back, gain_grad)

def scores_of(query, keys, bias, mask):
    rows = query.shape[0]
    q3 = query.reshape(rows, -1, HEAD)
    k3 = keys.reshape(keys.shape[0], -1, HEAD)
    scores = prod('qhd,khd->hqk', q3, k3)
    if bias is not None:
        scores = scores + bias
    if mask is not None:
        scores = jnp.where(mask[None], scores, -1e+30)
    return scores

def attend(query, keys, values, bias, mask, shifted):
    rows = query.shape[0]
    scores = scores_of(query, keys, bias, mask)
    if shifted:
        top = lax.optimization_barrier(jnp.max(scores, axis=-1, keepdims=True))
        lse = top + jnp.log(lax.optimization_barrier(jnp.sum(jnp.exp(scores - top), axis=-1, keepdims=True)))
    else:
        lse = jnp.log(lax.optimization_barrier(jnp.sum(jnp.exp(scores), axis=-1, keepdims=True)))
    prob = jnp.exp(scores - lse).astype(jnp.bfloat16)
    v3 = values.reshape(values.shape[0], -1, HEAD)
    out = prod('hqk,khd->qhd', prob, v3).reshape(rows, -1).astype(jnp.bfloat16)
    return (out, lse)

def attend_back(query, keys, values, out, lse, grad_out, bias, mask):
    rows = query.shape[0]
    scores = scores_of(query, keys, bias, mask)
    prob = jnp.exp(scores - lse)
    prob_b = prob.astype(jnp.bfloat16)
    q3 = query.reshape(rows, -1, HEAD)
    k3 = keys.reshape(keys.shape[0], -1, HEAD)
    v3 = values.reshape(values.shape[0], -1, HEAD)
    grad3 = grad_out.reshape(rows, -1, HEAD)
    grad_b = grad3.astype(jnp.bfloat16)
    out3 = out.reshape(rows, -1, HEAD).astype(jnp.float32)
    d_val = prod('hqk,qhd->khd', prob_b, grad_b)
    d_prob = prod('qhd,khd->hqk', grad_b, v3)
    delta = jnp.transpose(lax.optimization_barrier(jnp.sum(grad3 * out3, axis=2)), (1, 0))
    d_score = prob * (d_prob - delta[:, :, None])
    d_score_b = d_score.astype(jnp.bfloat16)
    d_query = prod('hqk,khd->qhd', d_score_b, k3)
    d_key = prod('hqk,qhd->khd', d_score_b, q3)
    shape_q = (rows, -1)
    shape_k = (keys.shape[0], -1)
    return (d_query.reshape(shape_q).astype(jnp.bfloat16), d_key.reshape(shape_k).astype(jnp.bfloat16), d_val.reshape(shape_k).astype(jnp.bfloat16), d_score)

def forward(rows, enc, length, bucket_ids, weights, table):
    qkv_w, out_w, ff_in, ff_out, gains = weights
    seq = rows.shape[0]
    gain_f = gains.astype(jnp.float32)
    start = rows.astype(jnp.float32)
    h1, n1, r1 = rms_fwd(start, gain_f[0])
    qkv = prod('ld,dce->cle', h1, qkv_w[:, 0:3]).astype(jnp.bfloat16)
    row_ids = lax.broadcasted_iota(jnp.int32, (seq, seq), 0)
    col_ids = lax.broadcasted_iota(jnp.int32, (seq, seq), 1)
    dist = jnp.maximum(row_ids - col_ids, 0)
    mask = (col_ids <= row_ids) & (col_ids < length)
    onehot = (bucket_ids[:, None] == jnp.arange(table.shape[0], dtype=jnp.int32)[None, :]).astype(jnp.float32)
    bias_dist = jnp.dot(onehot, table, precision=lax.Precision.HIGHEST)
    bias = jnp.transpose(bias_dist[dist], (2, 0, 1))
    a1, lse1 = attend(qkv[0], qkv[1], qkv[2], bias, mask, True)
    x1 = start + prod('le,ed->ld', a1, out_w[:, 0])
    h2, n2, r2 = rms_fwd(x1, gain_f[1])
    qc = prod('ld,de->le', h2, qkv_w[:, 3]).astype(jnp.bfloat16)
    kvc = prod('ld,dce->cle', enc, qkv_w[:, 4:6]).astype(jnp.bfloat16)
    ac, lse2 = attend(qc, kvc[0], kvc[1], None, None, False)
    x2 = x1 + prod('le,ed->ld', ac, out_w[:, 1])
    h3, n3, r3 = rms_fwd(x2, gain_f[2])
    gate_up = prod('ld,dcf->clf', h3, ff_in)
    hidden = (gelu_tanh(gate_up[0]) * gate_up[1]).astype(jnp.bfloat16)
    result = x2 + prod('lf,fd->ld', hidden, ff_out)
    saved = (h1, n1, r1, qkv, bias, mask, a1, lse1, h2, n2, r2, qc, kvc, ac, lse2, h3, n3, r3, gate_up, hidden, onehot, dist)
    return (result.astype(jnp.bfloat16), saved)

def ff_back(saved, weights, cot):
    qkv_w, out_w, ff_in, ff_out, gains = weights
    gain_f = gains.astype(jnp.float32)
    h3, n3, r3, gate_up, hidden = (saved[15], saved[16], saved[17], saved[18], saved[19])
    d_ffout = prod('lf,ld->fd', hidden, cot)
    d_hidden = prod('ld,fd->lf', cot, ff_out)
    gelu_val, gelu_pull = jax.vjp(gelu_tanh, gate_up[0])
    d_gate = gelu_pull(d_hidden * gate_up[1])[0]
    d_up = d_hidden * gelu_val
    d_gate_up = jnp.stack([d_gate, d_up]).astype(jnp.bfloat16)
    d_ffin = prod('ld,clf->dcf', h3, d_gate_up)
    d_h3 = prod('clf,dcf->ld', d_gate_up, ff_in)
    back3, gain3 = rms_bwd(d_h3, n3, r3, gain_f[2])
    return (cot.astype(jnp.float32) + back3, d_ffin, d_ffout, gain3)

def cross_back(saved, weights, enc, dx2):
    qkv_w, out_w, ff_in, ff_out, gains = weights
    gain_f = gains.astype(jnp.float32)
    h2, n2, r2, qc, kvc, ac, lse2 = (saved[8], saved[9], saved[10], saved[11], saved[12], saved[13], saved[14])
    dx2_b = dx2.astype(jnp.bfloat16)
    d_outc = prod('le,ld->ed', ac, dx2_b)
    d_ac = prod('ld,ed->le', dx2_b, out_w[:, 1])
    d_qc, d_kc, d_vc, unused = attend_back(qc, kvc[0], kvc[1], ac, lse2, d_ac, None, None)
    g_qc = prod('ld,le->de', h2, d_qc)
    d_kvc = jnp.stack([d_kc, d_vc])
    g_kvc = prod('ld,cle->dce', enc, d_kvc)
    enc_grad = prod('cle,dce->ld', d_kvc, qkv_w[:, 4:6]).astype(jnp.bfloat16)
    d_h2 = prod('le,de->ld', d_qc, qkv_w[:, 3])
    back2, gain2 = rms_bwd(d_h2, n2, r2, gain_f[1])
    return (dx2 + back2, g_qc, g_kvc, d_outc, gain2, enc_grad)

def self_back(saved, weights, dx1):
    qkv_w, out_w, ff_in, ff_out, gains = weights
    gain_f = gains.astype(jnp.float32)
    h1, n1, r1, qkv, bias, mask, a1, lse1 = saved[0:8]
    onehot, dist = (saved[20], saved[21])
    seq = h1.shape[0]
    dx1_b = dx1.astype(jnp.bfloat16)
    d_outs = prod('le,ld->ed', a1, dx1_b)
    d_a1 = prod('ld,ed->le', dx1_b, out_w[:, 0])
    d_q, d_k, d_v, d_score = attend_back(qkv[0], qkv[1], qkv[2], a1, lse1, d_a1, bias, mask)
    d_qkv = jnp.stack([d_q, d_k, d_v])
    g_qkv = prod('ld,cle->dce', h1, d_qkv)
    d_h1 = prod('cle,dce->ld', d_qkv, qkv_w[:, 0:3])
    back1, gain1 = rms_bwd(d_h1, n1, r1, gain_f[0])
    flat = jnp.transpose(d_score, (1, 2, 0)).reshape(seq * seq, -1)
    d_dist = jax.ops.segment_sum(flat, dist.reshape(-1), num_segments=seq)
    d_table = jnp.dot(onehot.T, d_dist, precision=lax.Precision.HIGHEST)
    return ((dx1 + back1).astype(jnp.bfloat16), g_qkv, d_outs, gain1, d_table)

def reference(inputs, encoded, lengths, bucket_ids, qkv_weights, out_weights, ff_in, ff_out, gains, bias_table, cotangent):
    weights = (qkv_weights, out_weights, ff_in, ff_out, gains)

    def one(carry, item):
        rows, enc, length, cot = item
        result, saved = forward(rows, enc, length, bucket_ids, weights, bias_table)
        dx2, g_ffin, g_ffout, gain3 = ff_back(saved, weights, cot)
        dx1, g_qc, g_kvc, g_outc, gain2, enc_grad = cross_back(saved, weights, enc, dx2)
        dx, g_qkvs, g_outs, gain1, g_table = self_back(saved, weights, dx1)
        g_qkv = jnp.concatenate([g_qkvs, g_qc[:, None], g_kvc], axis=1)
        g_out = jnp.stack([g_outs, g_outc], axis=1)
        g_gain = jnp.stack([gain1, gain2, gain3])
        terms = (g_qkv, g_out, g_ffin, g_ffout, g_gain, g_table)
        carry = tuple((c + t for c, t in zip(carry, terms)))
        return (carry, (result, dx, enc_grad))
    zeros = (jnp.zeros(qkv_weights.shape, jnp.float32), jnp.zeros(out_weights.shape, jnp.float32), jnp.zeros(ff_in.shape, jnp.float32), jnp.zeros(ff_out.shape, jnp.float32), jnp.zeros(gains.shape, jnp.float32), jnp.zeros(bias_table.shape, jnp.float32))
    totals, per_seq = lax.scan(one, zeros, (inputs, encoded, lengths, cotangent))
    outputs, input_grad, encoded_grad = per_seq
    return (outputs, input_grad, encoded_grad, totals[0], totals[1], totals[2], totals[3], totals[4], totals[5])
```

```python
import math

import jax
import jax.numpy as jnp
from jax import lax
from jax.sharding import PartitionSpec as P

HEAD = 64


EPS = 1e-06


def prod(form, left, right):
    return jnp.einsum(form, left, right, preferred_element_type=jnp.float32)


def gelu_tanh(value):
    return (
        0.5
        * value
        * (1.0 + jnp.tanh(0.7978845608028654 * (value + 0.044715 * value * value * value)))
    )


def rms_fwd(value, gain):
    recip = lax.rsqrt(jnp.mean(value * value, axis=-1, keepdims=True) + EPS)
    normed = value * recip
    return ((normed * gain).astype(jnp.bfloat16), normed, recip)


def rms_bwd(grad, normed, recip, gain):
    scaled = grad * gain
    gain_grad = jnp.sum(grad * normed, axis=0)
    back = recip * (scaled - normed * jnp.mean(scaled * normed, axis=-1, keepdims=True))
    return (back, gain_grad)


def toeplitz_bias(bucket_ids, table, positions):
    onehot = (bucket_ids[:, None] == jnp.arange(table.shape[0], dtype=jnp.int32)[None, :]).astype(
        jnp.float32
    )
    by_dist = jnp.transpose(jnp.dot(onehot, table, precision=lax.Precision.HIGHEST), (1, 0))
    head_count = by_dist.shape[0]
    nearest = jnp.broadcast_to(by_dist[:, 0:1], (head_count, positions))
    cyclic = jnp.concatenate(
        [nearest, jnp.zeros((head_count, 1), jnp.float32), by_dist[:, :0:-1]], axis=1
    )
    tiled = jnp.broadcast_to(cyclic[:, None, :], (head_count, positions, 2 * positions))
    tiled = tiled.reshape(head_count, 2 * positions * positions)
    skewed = tiled[:, : positions * (2 * positions - 1)].reshape(
        head_count, positions, 2 * positions - 1
    )
    return (skewed[:, :, :positions], onehot)


def diagonal_sums(d_score, onehot):
    head_count, positions = (d_score.shape[0], d_score.shape[1])
    padded = jnp.pad(d_score, ((0, 0), (0, 0), (0, positions - 1)))
    padded = padded.reshape(head_count, positions * (2 * positions - 1))
    padded = jnp.pad(padded, ((0, 0), (0, positions))).reshape(head_count, positions, 2 * positions)
    column = jnp.sum(padded, axis=1)
    by_dist = jnp.concatenate(
        [jnp.sum(column[:, :positions], axis=1, keepdims=True), column[:, :positions:-1]], axis=1
    )
    return jnp.dot(
        jnp.transpose(onehot, (1, 0)),
        jnp.transpose(by_dist, (1, 0)),
        precision=lax.Precision.HIGHEST,
    )


def scores_of(query, keys, bias, mask):
    rows = query.shape[0]
    q3 = query.reshape(rows, -1, HEAD)
    k3 = keys.reshape(keys.shape[0], -1, HEAD)
    scores = prod("qhd,khd->hqk", q3, k3)
    if bias is not None:
        scores = scores + bias
    if mask is not None:
        scores = jnp.where(mask[None], scores, -1e30)
    return scores


def attend(query, keys, values, bias, mask, shifted):
    rows = query.shape[0]
    scores = scores_of(query, keys, bias, mask)
    if shifted:
        top = jnp.max(scores, axis=-1, keepdims=True)
        lse = top + jnp.log(jnp.sum(jnp.exp(scores - top), axis=-1, keepdims=True))
    else:
        lse = jnp.log(jnp.sum(jnp.exp(scores), axis=-1, keepdims=True))
    prob = jnp.exp(scores - lse).astype(jnp.bfloat16)
    v3 = values.reshape(values.shape[0], -1, HEAD)
    out = prod("hqk,khd->qhd", prob, v3).reshape(rows, -1).astype(jnp.bfloat16)
    return (out, lse)


def attend_back(query, keys, values, out, lse, grad_out, bias, mask):
    rows = query.shape[0]
    scores = scores_of(query, keys, bias, mask)
    prob = jnp.exp(scores - lse)
    prob_b = prob.astype(jnp.bfloat16)
    q3 = query.reshape(rows, -1, HEAD)
    k3 = keys.reshape(keys.shape[0], -1, HEAD)
    v3 = values.reshape(values.shape[0], -1, HEAD)
    grad3 = grad_out.reshape(rows, -1, HEAD)
    grad_b = grad3.astype(jnp.bfloat16)
    out3 = out.reshape(rows, -1, HEAD).astype(jnp.float32)
    d_val = prod("hqk,qhd->khd", prob_b, grad_b)
    d_prob = prod("qhd,khd->hqk", grad_b, v3)
    delta = jnp.transpose(jnp.sum(grad3 * out3, axis=2), (1, 0))
    d_score = prob * (d_prob - delta[:, :, None])
    d_score_b = d_score.astype(jnp.bfloat16)
    d_query = prod("hqk,khd->qhd", d_score_b, k3)
    d_key = prod("hqk,qhd->khd", d_score_b, q3)
    shape_q = (rows, -1)
    shape_k = (keys.shape[0], -1)
    return (
        d_query.reshape(shape_q).astype(jnp.bfloat16),
        d_key.reshape(shape_k).astype(jnp.bfloat16),
        d_val.reshape(shape_k).astype(jnp.bfloat16),
        d_score,
    )


def forward(rows, enc, length, bucket_ids, weights, table):
    qkv_w, out_w, ff_in, ff_out, gains = weights
    positions = rows.shape[0]
    gain_f = gains.astype(jnp.float32)
    start = rows.astype(jnp.float32)
    h1, n1, r1 = rms_fwd(start, gain_f[0])
    qkv = prod("ld,cde->cle", h1, qkv_w[0:3]).astype(jnp.bfloat16)
    row_ids = lax.broadcasted_iota(jnp.int32, (positions, positions), 0)
    col_ids = lax.broadcasted_iota(jnp.int32, (positions, positions), 1)
    mask = (col_ids <= row_ids) & (col_ids < length)
    bias, onehot = toeplitz_bias(bucket_ids, table, positions)
    a1, lse1 = attend(qkv[0], qkv[1], qkv[2], bias, mask, True)
    x1 = start + prod("le,ed->ld", a1, out_w[0])
    h2, n2, r2 = rms_fwd(x1, gain_f[1])
    qc = prod("ld,de->le", h2, qkv_w[3]).astype(jnp.bfloat16)
    kvc = prod("ld,cde->cle", enc, qkv_w[4:6]).astype(jnp.bfloat16)
    ac, lse2 = attend(qc, kvc[0], kvc[1], None, None, False)
    x2 = x1 + prod("le,ed->ld", ac, out_w[1])
    h3, n3, r3 = rms_fwd(x2, gain_f[2])
    gate_up = prod("ld,cdf->clf", h3, ff_in)
    hidden = (gelu_tanh(gate_up[0]) * gate_up[1]).astype(jnp.bfloat16)
    result = x2 + prod("lf,fd->ld", hidden, ff_out)
    saved = (
        h1,
        n1,
        r1,
        qkv,
        bias,
        mask,
        a1,
        lse1,
        h2,
        n2,
        r2,
        qc,
        kvc,
        ac,
        lse2,
        h3,
        n3,
        r3,
        gate_up,
        hidden,
        onehot,
    )
    return (result.astype(jnp.bfloat16), saved)


def ff_back(saved, weights, cot):
    qkv_w, out_w, ff_in, ff_out, gains = weights
    gain_f = gains.astype(jnp.float32)
    h3, n3, r3, gate_up, hidden = (saved[15], saved[16], saved[17], saved[18], saved[19])
    d_ffout = prod("lf,ld->fd", hidden, cot)
    d_hidden = prod("ld,fd->lf", cot, ff_out)
    gelu_val, gelu_pull = jax.vjp(gelu_tanh, gate_up[0])
    d_gate = gelu_pull(d_hidden * gate_up[1])[0]
    d_up = d_hidden * gelu_val
    d_gate_up = jnp.stack([d_gate, d_up]).astype(jnp.bfloat16)
    d_ffin = prod("ld,clf->cdf", h3, d_gate_up)
    d_h3 = prod("clf,cdf->ld", d_gate_up, ff_in)
    back3, gain3 = rms_bwd(d_h3, n3, r3, gain_f[2])
    return (cot.astype(jnp.float32) + back3, d_ffin, d_ffout, gain3)


def cross_back(saved, weights, enc, dx2):
    qkv_w, out_w, ff_in, ff_out, gains = weights
    gain_f = gains.astype(jnp.float32)
    h2, n2, r2, qc, kvc, ac, lse2 = (
        saved[8],
        saved[9],
        saved[10],
        saved[11],
        saved[12],
        saved[13],
        saved[14],
    )
    dx2_b = dx2.astype(jnp.bfloat16)
    d_outc = prod("le,ld->ed", ac, dx2_b)
    d_ac = prod("ld,ed->le", dx2_b, out_w[1])
    d_qc, d_kc, d_vc, unused = attend_back(qc, kvc[0], kvc[1], ac, lse2, d_ac, None, None)
    g_qc = prod("ld,le->de", h2, d_qc)
    d_kvc = jnp.stack([d_kc, d_vc])
    g_kvc = prod("ld,cle->cde", enc, d_kvc)
    enc_grad = prod("cle,cde->ld", d_kvc, qkv_w[4:6]).astype(jnp.bfloat16)
    d_h2 = prod("le,de->ld", d_qc, qkv_w[3])
    back2, gain2 = rms_bwd(d_h2, n2, r2, gain_f[1])
    return (dx2 + back2, g_qc, g_kvc, d_outc, gain2, enc_grad)


def self_back(saved, weights, dx1):
    qkv_w, out_w, ff_in, ff_out, gains = weights
    gain_f = gains.astype(jnp.float32)
    h1, n1, r1, qkv, bias, mask, a1, lse1 = saved[0:8]
    onehot = saved[20]
    dx1_b = dx1.astype(jnp.bfloat16)
    d_outs = prod("le,ld->ed", a1, dx1_b)
    d_a1 = prod("ld,ed->le", dx1_b, out_w[0])
    d_q, d_k, d_v, d_score = attend_back(qkv[0], qkv[1], qkv[2], a1, lse1, d_a1, bias, mask)
    d_qkv = jnp.stack([d_q, d_k, d_v])
    g_qkv = prod("ld,cle->cde", h1, d_qkv)
    d_h1 = prod("cle,cde->ld", d_qkv, qkv_w[0:3])
    back1, gain1 = rms_bwd(d_h1, n1, r1, gain_f[0])
    d_table = diagonal_sums(d_score, onehot)
    return ((dx1 + back1).astype(jnp.bfloat16), g_qkv, d_outs, gain1, d_table)


def pack(arrays, width):
    blocks = []
    for array in arrays:
        for copy in range(array.shape[0]):
            for start in range(0, array.shape[-1], width):
                blocks.append(array[copy, :, :, start : start + width])
    return jnp.concatenate(blocks, axis=1)


def unpack(packed, shapes, width):
    count = packed.shape[0]
    arrays, row = [], 0
    for copies, rows, columns in shapes:
        planes = []
        for copy in range(copies):
            blocks = []
            for start in range(0, columns, width):
                blocks.append(packed[:, row : row + rows].reshape(count * rows, width))
                row += rows
            planes.append(jnp.concatenate(blocks, axis=1))
        arrays.append(jnp.stack(planes))
    return arrays


def per_device(
    inputs,
    encoded,
    lengths,
    bucket_ids,
    qkv_weights,
    out_weights,
    ff_in,
    ff_out,
    gains,
    bias_table,
    cotangent,
):
    count = lax.axis_size("fsdp")
    shards = (
        jnp.transpose(qkv_weights, (1, 0, 2)),
        jnp.transpose(out_weights, (1, 0, 2)),
        jnp.transpose(ff_in, (1, 0, 2)),
        ff_out[None],
    )
    width = math.gcd(qkv_weights.shape[-1], ff_in.shape[-1])
    packed = pack([shard[:, None] for shard in shards], width)
    slots = gains.size
    tail = -(-slots // width)
    gain_rows = jnp.pad(gains.reshape(1, slots), ((0, 0), (0, tail * width - slots)))
    packed = jnp.concatenate([packed, gain_rows.reshape(1, tail, width)], axis=1)
    whole = lax.all_gather(packed, "fsdp", axis=0, tiled=True)
    main = unpack(whole, [shard.shape for shard in shards], width)
    gain_all = whole[:, -tail:].reshape(count, tail * width)[:, :slots]
    gain_all = gain_all.reshape(count, gains.shape[0], gains.shape[1])
    gain_all = jnp.transpose(gain_all, (1, 0, 2)).reshape(gains.shape[0], -1)
    weights = (main[0], main[1], main[2], main[3][0], gain_all)
    result, saved = forward(inputs[0], encoded[0], lengths[0], bucket_ids, weights, bias_table)
    dx2, g_ffin, g_ffout, gain3 = ff_back(saved, weights, cotangent[0])
    dx1, g_qc, g_kvc, g_outc, gain2, enc_grad = cross_back(saved, weights, encoded[0], dx2)
    dx, g_qkvs, g_outs, gain1, g_table = self_back(saved, weights, dx1)
    grads = (
        [g_qkvs[0], g_qkvs[1], g_qkvs[2], g_qc, g_kvc[0], g_kvc[1]],
        [g_outs, g_outc],
        [g_ffin[0], g_ffin[1]],
        [g_ffout],
    )
    send = []
    for group in grads:
        for grad in group:
            send.append(grad.astype(jnp.bfloat16).reshape(1, count, -1, grad.shape[-1]))
    send = pack(send, width)
    g_gain = jnp.stack([gain1, gain2, gain3])
    send, g_gain, g_table = lax.optimization_barrier((send, g_gain, g_table))
    own = lax.psum_scatter(send, "fsdp", scatter_dimension=0, tiled=True)
    s_main = unpack(own, [shard.shape for shard in shards], width)
    s_main = [part.astype(jnp.float32) for part in s_main]
    s_gain = lax.psum_scatter(g_gain, "fsdp", scatter_dimension=1, tiled=True)
    s_table = lax.psum(g_table, "fsdp")
    return (
        result[None],
        dx[None],
        enc_grad[None],
        jnp.transpose(s_main[0], (1, 0, 2)),
        jnp.transpose(s_main[1], (1, 0, 2)),
        jnp.transpose(s_main[2], (1, 0, 2)),
        s_main[3][0],
        s_gain,
        s_table,
    )


def solution(mesh):
    placed = (
        P("fsdp", None, None),
        P("fsdp", None, None),
        P("fsdp"),
        P(),
        P("fsdp", None, None),
        P("fsdp", None, None),
        P("fsdp", None, None),
        P("fsdp", None),
        P(None, "fsdp"),
        P(),
        P("fsdp", None, None),
    )
    return jax.shard_map(
        per_device,
        mesh=mesh,
        in_specs=placed,
        out_specs=(
            P("fsdp", None, None),
            P("fsdp", None, None),
            P("fsdp", None, None),
            P("fsdp", None, None),
            P("fsdp", None, None),
            P("fsdp", None, None),
            P("fsdp", None),
            P(None, "fsdp"),
            P(),
        ),
        check_vma=False,
    )
```

```python
import jax
import jax.numpy as jnp
from jax import lax
from jax.sharding import PartitionSpec as P

HEAD = 64


EPS = 1e-06


def prod(form, left, right):
    return jnp.einsum(form, left, right, preferred_element_type=jnp.float32)


def gelu_tanh(value):
    return (
        0.5
        * value
        * (1.0 + jnp.tanh(0.7978845608028654 * (value + 0.044715 * value * value * value)))
    )


def rms_fwd(value, gain):
    recip = lax.rsqrt(jnp.mean(value * value, axis=-1, keepdims=True) + EPS)
    normed = value * recip
    return ((normed * gain).astype(jnp.bfloat16), normed, recip)


def rms_bwd(grad, normed, recip, gain):
    scaled = grad * gain
    gain_grad = jnp.sum(grad * normed, axis=0)
    back = recip * (scaled - normed * jnp.mean(scaled * normed, axis=-1, keepdims=True))
    return (back, gain_grad)


def toeplitz_bias(bucket_ids, table, positions):
    onehot = (bucket_ids[:, None] == jnp.arange(table.shape[0], dtype=jnp.int32)[None, :]).astype(
        jnp.float32
    )
    by_dist = jnp.transpose(jnp.dot(onehot, table, precision=lax.Precision.HIGHEST), (1, 0))
    head_count = by_dist.shape[0]
    nearest = jnp.broadcast_to(by_dist[:, 0:1], (head_count, positions))
    cyclic = jnp.concatenate(
        [nearest, jnp.zeros((head_count, 1), jnp.float32), by_dist[:, :0:-1]], axis=1
    )
    tiled = jnp.broadcast_to(cyclic[:, None, :], (head_count, positions, 2 * positions))
    tiled = tiled.reshape(head_count, 2 * positions * positions)
    skewed = tiled[:, : positions * (2 * positions - 1)].reshape(
        head_count, positions, 2 * positions - 1
    )
    return (skewed[:, :, :positions], onehot)


def diagonal_sums(d_score, onehot):
    head_count, positions = (d_score.shape[0], d_score.shape[1])
    padded = jnp.pad(d_score, ((0, 0), (0, 0), (0, positions - 1)))
    padded = padded.reshape(head_count, positions * (2 * positions - 1))
    padded = jnp.pad(padded, ((0, 0), (0, positions))).reshape(head_count, positions, 2 * positions)
    column = jnp.sum(padded, axis=1)
    by_dist = jnp.concatenate(
        [jnp.sum(column[:, :positions], axis=1, keepdims=True), column[:, :positions:-1]], axis=1
    )
    return jnp.dot(
        jnp.transpose(onehot, (1, 0)),
        jnp.transpose(by_dist, (1, 0)),
        precision=lax.Precision.HIGHEST,
    )


def scores_of(query, keys, bias, mask):
    rows = query.shape[0]
    q3 = query.reshape(rows, -1, HEAD)
    k3 = keys.reshape(keys.shape[0], -1, HEAD)
    scores = prod("qhd,khd->hqk", q3, k3)
    if bias is not None:
        scores = scores + bias
    if mask is not None:
        scores = jnp.where(mask[None], scores, -1e30)
    return scores


def attend(query, keys, values, bias, mask, shifted):
    rows = query.shape[0]
    scores = scores_of(query, keys, bias, mask)
    if shifted:
        top = jnp.max(scores, axis=-1, keepdims=True)
        lse = top + jnp.log(jnp.sum(jnp.exp(scores - top), axis=-1, keepdims=True))
    else:
        lse = jnp.log(jnp.sum(jnp.exp(scores), axis=-1, keepdims=True))
    prob = jnp.exp(scores - lse).astype(jnp.bfloat16)
    v3 = values.reshape(values.shape[0], -1, HEAD)
    out = prod("hqk,khd->qhd", prob, v3).reshape(rows, -1).astype(jnp.bfloat16)
    return (out, lse)


def attend_back(query, keys, values, out, lse, grad_out, bias, mask):
    rows = query.shape[0]
    scores = scores_of(query, keys, bias, mask)
    prob = jnp.exp(scores - lse)
    prob_b = prob.astype(jnp.bfloat16)
    q3 = query.reshape(rows, -1, HEAD)
    k3 = keys.reshape(keys.shape[0], -1, HEAD)
    v3 = values.reshape(values.shape[0], -1, HEAD)
    grad3 = grad_out.reshape(rows, -1, HEAD)
    grad_b = grad3.astype(jnp.bfloat16)
    out3 = out.reshape(rows, -1, HEAD).astype(jnp.float32)
    d_val = prod("hqk,qhd->khd", prob_b, grad_b)
    d_prob = prod("qhd,khd->hqk", grad_b, v3)
    delta = jnp.transpose(jnp.sum(grad3 * out3, axis=2), (1, 0))
    d_score = prob * (d_prob - delta[:, :, None])
    d_score_b = d_score.astype(jnp.bfloat16)
    d_query = prod("hqk,khd->qhd", d_score_b, k3)
    d_key = prod("hqk,qhd->khd", d_score_b, q3)
    shape_q = (rows, -1)
    shape_k = (keys.shape[0], -1)
    return (
        d_query.reshape(shape_q).astype(jnp.bfloat16),
        d_key.reshape(shape_k).astype(jnp.bfloat16),
        d_val.reshape(shape_k).astype(jnp.bfloat16),
        d_score,
    )


def forward(rows, enc, length, bucket_ids, weights, table):
    qkv_w, out_w, ff_in, ff_out, gains = weights
    positions = rows.shape[0]
    gain_f = gains.astype(jnp.float32)
    start = rows.astype(jnp.float32)
    h1, n1, r1 = rms_fwd(start, gain_f[0])
    qkv = prod("ld,cde->cle", h1, qkv_w[0:3]).astype(jnp.bfloat16)
    row_ids = lax.broadcasted_iota(jnp.int32, (positions, positions), 0)
    col_ids = lax.broadcasted_iota(jnp.int32, (positions, positions), 1)
    mask = (col_ids <= row_ids) & (col_ids < length)
    bias, onehot = toeplitz_bias(bucket_ids, table, positions)
    a1, lse1 = attend(qkv[0], qkv[1], qkv[2], bias, mask, True)
    x1 = start + prod("le,ed->ld", a1, out_w[0])
    h2, n2, r2 = rms_fwd(x1, gain_f[1])
    qc = prod("ld,de->le", h2, qkv_w[3]).astype(jnp.bfloat16)
    kvc = prod("ld,cde->cle", enc, qkv_w[4:6]).astype(jnp.bfloat16)
    ac, lse2 = attend(qc, kvc[0], kvc[1], None, None, False)
    x2 = x1 + prod("le,ed->ld", ac, out_w[1])
    h3, n3, r3 = rms_fwd(x2, gain_f[2])
    gate_up = prod("ld,cdf->clf", h3, ff_in)
    hidden = (gelu_tanh(gate_up[0]) * gate_up[1]).astype(jnp.bfloat16)
    result = x2 + prod("lf,fd->ld", hidden, ff_out)
    saved = (
        h1,
        n1,
        r1,
        qkv,
        bias,
        mask,
        a1,
        lse1,
        h2,
        n2,
        r2,
        qc,
        kvc,
        ac,
        lse2,
        h3,
        n3,
        r3,
        gate_up,
        hidden,
        onehot,
    )
    return (result.astype(jnp.bfloat16), saved)


def ff_back(saved, weights, cot):
    qkv_w, out_w, ff_in, ff_out, gains = weights
    gain_f = gains.astype(jnp.float32)
    h3, n3, r3, gate_up, hidden = (saved[15], saved[16], saved[17], saved[18], saved[19])
    d_ffout = prod("lf,ld->fd", hidden, cot)
    d_hidden = prod("ld,fd->lf", cot, ff_out)
    gelu_val, gelu_pull = jax.vjp(gelu_tanh, gate_up[0])
    d_gate = gelu_pull(d_hidden * gate_up[1])[0]
    d_up = d_hidden * gelu_val
    d_gate_up = jnp.stack([d_gate, d_up]).astype(jnp.bfloat16)
    d_ffin = prod("ld,clf->cdf", h3, d_gate_up)
    d_h3 = prod("clf,cdf->ld", d_gate_up, ff_in)
    back3, gain3 = rms_bwd(d_h3, n3, r3, gain_f[2])
    return (cot.astype(jnp.float32) + back3, d_ffin, d_ffout, gain3)


def cross_back(saved, weights, enc, dx2):
    qkv_w, out_w, ff_in, ff_out, gains = weights
    gain_f = gains.astype(jnp.float32)
    h2, n2, r2, qc, kvc, ac, lse2 = (
        saved[8],
        saved[9],
        saved[10],
        saved[11],
        saved[12],
        saved[13],
        saved[14],
    )
    dx2_b = dx2.astype(jnp.bfloat16)
    d_outc = prod("le,ld->ed", ac, dx2_b)
    d_ac = prod("ld,ed->le", dx2_b, out_w[1])
    d_qc, d_kc, d_vc, unused = attend_back(qc, kvc[0], kvc[1], ac, lse2, d_ac, None, None)
    g_qc = prod("ld,le->de", h2, d_qc)
    d_kvc = jnp.stack([d_kc, d_vc])
    g_kvc = prod("ld,cle->cde", enc, d_kvc)
    enc_grad = prod("cle,cde->ld", d_kvc, qkv_w[4:6]).astype(jnp.bfloat16)
    d_h2 = prod("le,de->ld", d_qc, qkv_w[3])
    back2, gain2 = rms_bwd(d_h2, n2, r2, gain_f[1])
    return (dx2 + back2, g_qc, g_kvc, d_outc, gain2, enc_grad)


def self_back(saved, weights, dx1):
    qkv_w, out_w, ff_in, ff_out, gains = weights
    gain_f = gains.astype(jnp.float32)
    h1, n1, r1, qkv, bias, mask, a1, lse1 = saved[0:8]
    onehot = saved[20]
    dx1_b = dx1.astype(jnp.bfloat16)
    d_outs = prod("le,ld->ed", a1, dx1_b)
    d_a1 = prod("ld,ed->le", dx1_b, out_w[0])
    d_q, d_k, d_v, d_score = attend_back(qkv[0], qkv[1], qkv[2], a1, lse1, d_a1, bias, mask)
    d_qkv = jnp.stack([d_q, d_k, d_v])
    g_qkv = prod("ld,cle->cde", h1, d_qkv)
    d_h1 = prod("cle,cde->ld", d_qkv, qkv_w[0:3])
    back1, gain1 = rms_bwd(d_h1, n1, r1, gain_f[0])
    d_table = diagonal_sums(d_score, onehot)
    return ((dx1 + back1).astype(jnp.bfloat16), g_qkv, d_outs, gain1, d_table)


def to_blocks(array, width):
    blocks = []
    for copy in range(array.shape[0]):
        for start in range(0, array.shape[-1], width):
            block = array[copy, ..., start : start + width]
            short = width - block.shape[-1]
            if short:
                block = jnp.pad(block, ((0, 0),) * (block.ndim - 1) + ((0, short),))
            blocks.append(block)
    return blocks


def from_blocks(blocks, shape, width):
    copies, rows, columns = shape
    each = -(-columns // width)
    planes = []
    for copy in range(copies):
        part = [blocks[copy * each + at] for at in range(each)]
        part[-1] = part[-1][..., : columns - (each - 1) * width]
        planes.append(part[0] if each == 1 else jnp.concatenate(part, axis=-1))
    return planes


def per_device(
    inputs,
    encoded,
    lengths,
    bucket_ids,
    qkv_weights,
    out_weights,
    ff_in,
    ff_out,
    gains,
    bias_table,
    cotangent,
):
    count = lax.axis_size("fsdp")
    shards = (
        jnp.transpose(qkv_weights, (1, 0, 2)),
        jnp.transpose(out_weights, (1, 0, 2)),
        jnp.transpose(ff_in, (1, 0, 2)),
        ff_out[None],
    )
    width = qkv_weights.shape[-1]
    depth = qkv_weights.shape[0]
    tall = ff_out.shape[0]
    blocks = to_blocks(shards[0], width) + to_blocks(shards[1], width) + to_blocks(shards[2], width)
    slots = gains.size
    tail = 8 * -(-slots // (8 * width))
    gain_rows = jnp.pad(gains.reshape(1, slots), ((0, 0), (0, tail * width - slots)))
    packed = jnp.concatenate(blocks + [ff_out, gain_rows.reshape(tail, width)], axis=0)
    whole = lax.all_gather(packed, "fsdp", axis=0, tiled=False)
    cut = len(blocks) * depth
    stacked = whole[:, :cut].reshape(count, len(blocks), depth, width)
    stacked = jnp.transpose(stacked, (1, 0, 2, 3)).reshape(len(blocks), count * depth, width)
    ff_out_all = whole[:, cut : cut + tall].reshape(count * tall, width)
    stacked, ff_out_all = lax.optimization_barrier((stacked, ff_out_all))
    n_qkv, n_out = qkv_weights.shape[1], out_weights.shape[1]
    ff_all = jnp.stack(from_blocks(stacked[n_qkv + n_out :], shards[2].shape, width))
    main = (stacked[:n_qkv], stacked[n_qkv : n_qkv + n_out], ff_all, ff_out_all[None])
    gain_all = whole[:, -tail:].reshape(count, tail * width)[:, :slots]
    gain_all = gain_all.reshape(count, gains.shape[0], gains.shape[1])
    gain_all = jnp.transpose(gain_all, (1, 0, 2)).reshape(gains.shape[0], -1)
    weights = (main[0], main[1], main[2], main[3][0], gain_all)
    result, saved = forward(inputs[0], encoded[0], lengths[0], bucket_ids, weights, bias_table)
    dx2, g_ffin, g_ffout, gain3 = ff_back(saved, weights, cotangent[0])
    dx1, g_qc, g_kvc, g_outc, gain2, enc_grad = cross_back(saved, weights, encoded[0], dx2)
    dx, g_qkvs, g_outs, gain1, g_table = self_back(saved, weights, dx1)
    wide = [g_qkvs[0], g_qkvs[1], g_qkvs[2], g_qc, g_kvc[0], g_kvc[1], g_outs, g_outc]
    wide += to_blocks(g_ffin, width)
    wide.append(g_ffout)
    g_gain = jnp.stack([gain1, gain2, gain3]).reshape(gains.shape[0], count, -1)
    g_gain = jnp.transpose(g_gain, (1, 0, 2)).reshape(count, slots)
    g_gain = jnp.pad(g_gain, ((0, 0), (0, tail * width - slots))).reshape(count, tail, width)
    parts = [grad.astype(jnp.bfloat16).reshape(count, -1, width) for grad in wide]
    send = jnp.concatenate(parts + [g_gain.astype(jnp.bfloat16)], axis=1)
    send, g_table = lax.optimization_barrier((send, g_table))
    own = lax.psum_scatter(send, "fsdp", scatter_dimension=0, tiled=False).astype(jnp.float32)
    mine = own[:cut].reshape(len(blocks), depth, width)
    s_ffin = jnp.stack(from_blocks(mine[n_qkv + n_out :], shards[2].shape, width))
    s_main = (mine[:n_qkv], mine[n_qkv : n_qkv + n_out], s_ffin, own[cut : cut + tall][None])
    s_gain = own[-tail:].reshape(tail * width)[:slots].reshape(gains.shape)
    s_table = lax.psum(g_table, "fsdp")
    return (
        result[None],
        dx[None],
        enc_grad[None],
        jnp.transpose(s_main[0], (1, 0, 2)),
        jnp.transpose(s_main[1], (1, 0, 2)),
        jnp.transpose(s_main[2], (1, 0, 2)),
        s_main[3][0],
        s_gain,
        s_table,
    )


def solution(mesh):
    placed = (
        P("fsdp", None, None),
        P("fsdp", None, None),
        P("fsdp"),
        P(),
        P("fsdp", None, None),
        P("fsdp", None, None),
        P("fsdp", None, None),
        P("fsdp", None),
        P(None, "fsdp"),
        P(),
        P("fsdp", None, None),
    )
    return jax.shard_map(
        per_device,
        mesh=mesh,
        in_specs=placed,
        out_specs=(
            P("fsdp", None, None),
            P("fsdp", None, None),
            P("fsdp", None, None),
            P("fsdp", None, None),
            P("fsdp", None, None),
            P("fsdp", None, None),
            P("fsdp", None),
            P(None, "fsdp"),
            P(),
        ),
        check_vma=False,
    )
```
